32 devices in a mesh: rep: 16 (over z, x, core), fsdp: 2 (over y).
Axes of the slice: x: 2, y: 2, z: 4, core: 2. Of those that a mesh axis runs over, the one named last changes fastest.
Arguments:
- hidden: bfloat16 [4096, 8192], P(('rep', 'fsdp')), may hold values from -6 to 6
- local_weight: bfloat16 [16, 8192, 2048], P('rep', 'fsdp'), may hold values from -0.09375 to 0.09375
- master: float32 [8192, 2048], P('fsdp', 'rep'), may hold values from -0.0625 to 0.0625
- momentum: float32 [8192, 2048], P('fsdp', 'rep'), may hold values from -0.06 to 0.06
- dither: int32 [16, 8192, 16], P('rep', 'fsdp'), may hold values from 0 to 15
Outputs:
- key_values: bfloat16 [4096, 2048], P(('rep', 'fsdp'))
- new_master: float32 [8192, 2048], P('fsdp', 'rep')
- new_momentum: float32 [8192, 2048], P('fsdp', 'rep')
- new_local: bfloat16 [16, 8192, 2048], P('rep', 'fsdp')
The draws below stay inside these ranges and needn't reach their ends.
All inputs are finite; a program needn't handle non-finite values.
Results may differ from the reference program's by a relative error of at most 0.0067.
Values may be sent and summed in bfloat16 or wider, within the bound.
No kernel may reach another device: no remote copies, remote signals or barrier semaphores. Data moves between devices by JAX's collectives and lax.ppermute only.
A program may use at most 192 MiB of HBM per device.

```python
import math
import jax
import jax.numpy as jnp
from jax import lax

D = 8192
BLOCK = 128
KVW = 2048
TOKENS = 4096
N_REP = 16


def place_ends(array, rng, smallest, largest):
    place = [jax.random.randint(jax.random.fold_in(rng, axis), (), 0, length) for axis, length in enumerate(array.shape)]
    widest = array.shape.index(max(array.shape))
    beside = place[:widest] + [(place[widest] + 1) % array.shape[widest]] + place[widest + 1:]
    return array.at[tuple(place)].set(smallest).at[tuple(beside)].set(largest)


def strengthened(drawn, stream_key, source, target, blocks, factor):
    def block_of(dim):
        return (jnp.arange(drawn.shape[dim]) // (drawn.shape[dim] // blocks)).reshape((-1,) + (1,) * (drawn.ndim - 1 - dim))

    first = jax.random.permutation(stream_key, blocks)[block_of(target)]
    second = (block_of(target) + blocks // 2) % blocks
    return jnp.where((block_of(source) == first) | (block_of(source) == second), factor * drawn, drawn)


def shard_levels(key, extent, split, least, largest):
    def one(dim, shards_of):
        draws = jax.random.uniform(jax.random.fold_in(jax.random.fold_in(key, 6), dim), (shards_of,), jnp.float32, least / len(split), largest / len(split))
        return jnp.repeat(jnp.exp(draws), extent[dim] // shards_of).reshape((-1,) + (1,) * (len(extent) - dim - 1))

    level = one(*split[0])
    for cut in split[1:]:
        level = level * one(*cut)
    return level


def centred(own_key, shape, deviation, most, cuts=(), held_as=jnp.bfloat16):
    array = deviation * jax.random.normal(own_key, shape, jnp.float32)
    if cuts:
        array = array * shard_levels(own_key, shape, cuts, -0.22, 0.18)
    return jnp.clip(array, -most, most).astype(held_as)


def bell_draw_with(stream_key, extent, spread, reach, pieces, heavy, dtype=jnp.bfloat16):
    values = spread * jax.random.normal(stream_key, extent, jnp.float32)
    if pieces:
        values = values * shard_levels(stream_key, extent, pieces, -0.22, 0.18)
    return jnp.clip(strengthened(values, jax.random.fold_in(stream_key, 3), *heavy), -reach, reach).astype(dtype)


def setup_inputs(seed: int = 0) -> dict:
    key_list = jax.random.split(jax.random.key(seed), 6)
    return {
        "hidden": centred(key_list[0], (TOKENS, D), 1.0, 6.0, ((0, 32),)),
        "local_weight": bell_draw_with(key_list[1], (N_REP, D, KVW), D ** -0.5, 0.09375, ((0, 16), (1, 2)), (0, 2, 16, 2.0)),
        "master": centred(key_list[2], (D, KVW), D ** -0.5, 0.0625, ((0, 2), (1, 16)), jnp.float32),
        "momentum": centred(key_list[3], (D, KVW), 0.01, 0.06, ((0, 2), (1, 16)), jnp.float32),
        "dither": place_ends(jax.random.randint(key_list[4], (N_REP, D, KVW // BLOCK), 0, 16), jax.random.fold_in(key_list[4], 1), 0, 15).astype(jnp.int32),
    }


momentum_keep = 0.9
outer_rate = 0.7
mix_share = 0.5


def code_block(delta, dither):
    row_count = delta.shape[0]
    blocked = delta.reshape(row_count, -1, BLOCK)
    scaling = (jnp.max(jnp.abs(blocked), axis=2, keepdims=True) + 1e-6) / 7.0
    offset = (dither.astype(jnp.float32)[:, :, None] + 0.5) / 16.0 - 0.5
    levels = jnp.clip(blocked / scaling + offset, -8.0, 7.0)
    smooth = levels - jnp.sin(2.0 * math.pi * levels) / (2.0 * math.pi)
    return (scaling * (smooth - offset)).reshape(row_count, -1)


def reference(hidden, local_weight, master, momentum, dither):
    anchor = lax.optimization_barrier(master.astype(jnp.bfloat16)).astype(jnp.float32)

    def accumulate(summed, pair_items):
        weights, offsets = pair_items
        coded = code_block(anchor - weights.astype(jnp.float32), offsets).astype(jnp.bfloat16)
        return summed + lax.optimization_barrier(coded).astype(jnp.float32), None

    summed, _ = lax.scan(accumulate, jnp.zeros(master.shape, jnp.float32), (local_weight, dither))
    averaged = summed / N_REP
    new_momentum = momentum_keep * momentum + averaged
    new_master = master - outer_rate * (averaged + momentum_keep * new_momentum)
    rounded = lax.optimization_barrier(new_master.astype(jnp.bfloat16)).astype(jnp.float32)

    def merge_one(weights):
        return (mix_share * weights.astype(jnp.float32) + (1.0 - mix_share) * rounded).astype(jnp.bfloat16)

    new_local = lax.map(merge_one, local_weight)
    grouped = hidden.reshape(N_REP, -1, D)

    def project(pair_items):
        return jnp.dot(pair_items[0], pair_items[1], preferred_element_type=jnp.float32).astype(jnp.bfloat16)

    key_values = lax.map(project, (grouped, local_weight)).reshape(-1, KVW)
    return key_values, new_master, new_momentum, new_local
```

```python
import functools
import math

import jax
import jax.numpy as jnp
from jax import lax
from jax.experimental import pallas as pl
from jax.experimental.pallas import tpu as pltpu
from jax.sharding import PartitionSpec as P

BLOCK = 128
momentum_keep = 0.9
outer_rate = 0.7
mix_share = 0.5

RESIDUE = (
    6.579736255284624,
    -12.98787530573671,
    12.207952703195676,
    -6.691029741717024,
    2.3803828656044055,
    -0.5278879155971964,
)

CHUNKS = 4
TILE = 256
STRIP = 16
MERGE_TILE = 256


def f32(array):
    return array.astype(jnp.float32)


def coded_strip(anchor, weights, offset):
    delta = anchor - f32(weights)
    scaling = (jnp.max(jnp.abs(delta), axis=1, keepdims=True) + 1e-06) * (1.0 / 7.0)
    levels = jnp.clip(delta * (1.0 / scaling) + offset, -8.0, 7.0)
    whole = jnp.round(levels)
    rest = levels - whole
    square = rest * rest
    q = jnp.full_like(square, RESIDUE[-1])
    for coefficient in RESIDUE[-2::-1]:
        q = q * square + coefficient
    smooth = whole + rest * square * q
    return f32((scaling * (smooth - offset)).astype(jnp.bfloat16))


def code_kernel(where_ref, anchor_ref, *refs, strip, first):
    slots, tile, width = anchor_ref.shape
    own_refs, mate_refs = refs[:slots], refs[slots : 2 * slots]
    own_off, mate_off, out_ref, own_wide, mate_wide = refs[2 * slots :]
    per = width // BLOCK
    blocks = own_off.shape[1]
    lane_block = lax.broadcasted_iota(jnp.int32, (blocks, width), 1) // BLOCK
    block = lax.broadcasted_iota(jnp.int32, (blocks, width), 0)
    for s in range(slots):
        pick = (block == lane_block + (first + s * per)).astype(jnp.bfloat16)
        own_wide[s] = jnp.dot(own_off[...], pick, preferred_element_type=jnp.float32)
        mate_wide[s] = jnp.dot(mate_off[...], pick, preferred_element_type=jnp.float32)

    def step(i, carry):
        rows = pl.ds(pl.multiple_of(i * strip, strip), strip)
        for s in range(slots):
            for b in range(per):
                lanes = slice(b * BLOCK, (b + 1) * BLOCK)
                anchor = f32(anchor_ref[s, rows, lanes])
                total = coded_strip(anchor, own_refs[s][rows, lanes], own_wide[s, rows, lanes])
                total += coded_strip(anchor, mate_refs[s][rows, lanes], mate_wide[s, rows, lanes])
                out_ref[s, rows, lanes] = total.astype(out_ref.dtype)
        return carry

    lax.fori_loop(0, tile // strip, step, 0)


def code(where, anchor, weights, mate, own_off, mate_off, group, row):
    slots, rows, width = anchor.shape
    half = weights.shape[0] // 2
    tile = min(TILE, rows)
    strip = min(STRIP, tile)
    blocks = own_off.shape[1]
    row_of = lambda i, w: w[0] * (half // tile) + row // tile + i
    column = lambda s: 1 + group * slots + s
    in_specs = [pl.BlockSpec((slots, tile, width), lambda i, w: (0, i, 0))]
    in_specs += [pl.BlockSpec((tile, width), lambda i, w, s=s: (row_of(i, w), w[column(s)])) for s in range(slots)]
    in_specs += [pl.BlockSpec((tile, width), lambda i, w, s=s: (i, w[column(s)])) for s in range(slots)]
    in_specs += [
        pl.BlockSpec((tile, blocks), lambda i, w: (row_of(i, w), 0)),
        pl.BlockSpec((tile, blocks), lambda i, w: (row // tile + i, 0)),
    ]
    return pl.pallas_call(
        functools.partial(code_kernel, strip=strip, first=group * slots * (width // BLOCK)),
        out_shape=jax.ShapeDtypeStruct(anchor.shape, jnp.bfloat16),
        grid_spec=pltpu.PrefetchScalarGridSpec(
            num_scalar_prefetch=1,
            grid=(rows // tile,),
            in_specs=in_specs,
            out_specs=pl.BlockSpec((slots, tile, width), lambda i, w: (0, i, 0)),
            scratch_shapes=[pltpu.VMEM((slots, tile, width), jnp.float32)] * 2,
        ),
        name="code_pair",
        compiler_params=pltpu.CompilerParams(dimension_semantics=("arbitrary",)),
        cost_estimate=pl.CostEstimate(flops=80 * anchor.size, transcendentals=0, bytes_accessed=8 * anchor.size),
    )(where, anchor, *([weights] * slots), *([mate] * slots), own_off, mate_off)


def merge_kernel(where_ref, *refs, groups):
    fresh, weights_ref, out_ref = refs[:groups], refs[groups], refs[-1]
    slots, _, width = fresh[0].shape
    for g in range(groups):
        for s in range(slots):
            lanes = pl.ds(pl.multiple_of(where_ref[1 + g * slots + s] * width, width), width)
            both = f32(weights_ref[:, lanes]) * mix_share + f32(fresh[g][s]) * (1.0 - mix_share)
            out_ref[:, lanes] = both.astype(out_ref.dtype)


def merge(where, fresh, weights, row, mine, so_far):
    slots, rows, width = fresh[0].shape
    half = weights.shape[0] // 2
    tile = min(MERGE_TILE, rows)

    def place(i, w):
        return ((w[0] if mine else 1 - w[0]) * (half // tile) + row // tile + i, 0)

    full = pl.BlockSpec((tile, weights.shape[1]), place)
    operands = [where, *fresh, weights]
    in_specs = [pl.BlockSpec((slots, tile, width), lambda i, w: (0, i, 0))] * len(fresh) + [full]
    aliases = {}
    if so_far is not None:
        aliases = {len(operands): 0}
        operands.append(so_far)
        in_specs.append(pl.BlockSpec(memory_space=pl.ANY))
    return pl.pallas_call(
        functools.partial(merge_kernel, groups=len(fresh)),
        out_shape=jax.ShapeDtypeStruct(weights.shape, jnp.bfloat16),
        grid_spec=pltpu.PrefetchScalarGridSpec(
            num_scalar_prefetch=1, grid=(rows // tile,), in_specs=in_specs, out_specs=full
        ),
        input_output_aliases=aliases,
        name="merge_rows",
        compiler_params=pltpu.CompilerParams(dimension_semantics=("arbitrary",)),
        cost_estimate=pl.CostEstimate(
            flops=4 * rows * weights.shape[1], transcendentals=0, bytes_accessed=6 * rows * weights.shape[1]
        ),
    )(*operands)


class Line:
    def __init__(self, total, length, stride):
        self.length = length
        self.stride = stride
        self.position = (lax.axis_index("rep") // stride) % length
        self.total = total

    def send(self, array, by):
        def target(i):
            n = (i // self.stride) % self.length
            return i + ((n + by) % self.length - n) * self.stride

        return lax.ppermute(array, "rep", [(i, target(i)) for i in range(self.total)])

    def gather(self, array):
        return [array] + [self.send(array, -d) for d in range(1, self.length)]

    def reduce(self, slots):
        arrived = [self.send(slots[d], d) for d in range(1, self.length)]
        return sum((f32(a) for a in arrived), f32(slots[0]))


def project(hidden, weights):
    share = lax.axis_size("fsdp")
    place = lax.axis_index("fsdp")
    depth = weights.shape[0]
    tokens = hidden.shape[0]

    def columns(at):
        return lax.dynamic_slice(hidden, (0, at % share * depth), (tokens, depth))

    def shifted(array, by):
        return lax.ppermute(array, "fsdp", [(i, (i + by) % share) for i in range(share)])

    gathered = [columns(place)] + [shifted(columns(place + s), s) for s in range(1, share)]
    partial = jnp.dot(jnp.concatenate(gathered), weights, preferred_element_type=jnp.float32)
    total = partial[:tokens]
    for s in range(1, share):
        total += shifted(partial[s * tokens : (s + 1) * tokens], -s)
    return total.astype(jnp.bfloat16)


def shards(hidden, local_weight, master, momentum, dither):
    weights = local_weight[0]
    rows, columns = weights.shape
    replicas = lax.axis_size("rep")
    chips = replicas // 2
    x_length = 2 ** int(math.log2(chips) / 2)
    z_length = chips // x_length
    core = lax.axis_index("rep") % 2
    x_line = Line(replicas, x_length, 2)
    z_line = Line(replicas, z_length, 2 * x_length)
    half = rows // 2
    piece = half // CHUNKS
    width = columns // chips
    mine, theirs = core * half, (1 - core) * half

    def swap(array):
        return lax.ppermute(array, "rep", [(i, i ^ 1) for i in range(replicas)])

    def halves(array, start, count=half):
        return lax.dynamic_slice(array, (start, 0), (count, array.shape[1]))

    def beside(own, other):
        return jnp.where(core == 0, jnp.concatenate([own, other], 1), jnp.concatenate([other, own], 1))

    rounded = master.astype(jnp.bfloat16)
    anchor = beside(halves(rounded, mine), swap(halves(rounded, theirs)))
    parts = [slice(i * piece, (i + 1) * piece) for i in range(CHUNKS)]

    groups = []
    for part in parts:
        pieces = z_line.gather(anchor[part])
        groups.append(x_line.gather(jnp.stack(pieces)))

    d = jnp.arange(z_length, dtype=jnp.int32)[None, :]
    e = jnp.arange(x_length, dtype=jnp.int32)[:, None]
    places = (((z_line.position + d) % z_length) * x_length + (x_line.position + e) % x_length).reshape(-1)
    where = jnp.concatenate([core[None].astype(jnp.int32), places])

    offset = (f32(dither[0]) + 0.5) / 16.0 - 0.5
    block_places = (places[:, None] * (width // BLOCK) + jnp.arange(width // BLOCK)[None, :]).reshape(-1)
    pick = jnp.arange(offset.shape[1])[:, None] == block_places[None, :]
    offset = jnp.dot(offset.astype(jnp.bfloat16), pick.astype(jnp.bfloat16), preferred_element_type=jnp.float32)
    offset = offset.astype(jnp.bfloat16)
    mate_offset = swap(halves(offset, theirs))
    mates = [swap(halves(weights, theirs + i * piece, piece)) for i in range(CHUNKS)]
    pair_master = beside(halves(master, mine), swap(halves(master, theirs)))
    pair_momentum = beside(halves(momentum, mine), swap(halves(momentum, theirs)))
    key_values = project(hidden, weights)

    masters, momenta, fresh, swapped = [], [], [], []
    for i, part in enumerate(parts):
        sums = [None] * x_length
        for g in reversed(range(x_length)):
            sums[g] = code(where, groups[i][g], weights, mates[i], offset, mate_offset, g, i * piece)
        summed = x_line.reduce(sums).astype(jnp.bfloat16)
        averaged = z_line.reduce([summed[k] for k in range(z_length)]) / replicas
        old_master, old_momentum, *_ = lax.optimization_barrier((pair_master[part], pair_momentum[part], *masters[-1:]))
        new_momentum = momentum_keep * old_momentum + averaged
        new_master = old_master - outer_rate * (averaged + momentum_keep * new_momentum)
        masters.append(new_master)
        momenta.append(new_momentum)
        pieces = z_line.gather(new_master.astype(jnp.bfloat16))
        fresh.append(x_line.gather(jnp.stack(pieces)))
        swapped.append([swap(group) for group in fresh[-1]])

    def home(pieces):
        pair = jnp.concatenate(pieces)
        own = pair.shape[1] // 2
        left, right = pair[:, :own], pair[:, own:]
        keep, give = jnp.where(core == 0, left, right), jnp.where(core == 0, right, left)
        got = swap(give)
        return jnp.where(core == 0, jnp.concatenate([keep, got]), jnp.concatenate([got, keep]))

    final_master, final_momentum = home(masters), home(momenta)
    new_local = None
    for i in range(CHUNKS + 1):
        if i < CHUNKS:
            new_local = merge(where, fresh[i], weights, i * piece, True, new_local)
        if i > 0:
            new_local = merge(where, swapped[i - 1], weights, (i - 1) * piece, False, new_local)
    return (key_values, final_master, final_momentum, new_local[None])


def solution(mesh):
    return jax.shard_map(
        shards,
        mesh=mesh,
        in_specs=(
            P(("rep", "fsdp"), None),
            P("rep", "fsdp", None),
            P("fsdp", "rep"),
            P("fsdp", "rep"),
            P("rep", "fsdp", None),
        ),
        out_specs=(
            P(("rep", "fsdp"), None),
            P("fsdp", "rep"),
            P("fsdp", "rep"),
            P("rep", "fsdp", None),
        ),
        check_vma=False,
    )
```

```python
import functools
import math

import jax
import jax.numpy as jnp
from jax import lax
from jax.experimental import pallas as pl
from jax.experimental.pallas import tpu as pltpu
from jax.sharding import PartitionSpec as P

BLOCK = 128
momentum_keep = 0.9
outer_rate = 0.7
mix_share = 0.5

RESIDUE = (6.579735248418329, -12.987673932477895, 12.201508758913876, -6.6188575657590425, 2.0504529183602735)

SHARES = (1, 1, 1, 1)
CHUNKS = len(SHARES)
TILE = 256
STRIP = 32
MERGE_TILE = 256


def f32(array):
    return array.astype(jnp.float32)


def coded_strip(anchor, weights, offset):
    delta = anchor - f32(weights)
    scaling = (jnp.max(jnp.abs(delta), axis=1, keepdims=True) + 1e-06) * (1.0 / 7.0)
    levels = jnp.clip(delta * (1.0 / scaling) + offset, -8.0, 7.0)
    whole = jnp.round(levels)
    rest = levels - whole
    square = rest * rest
    q = jnp.full_like(square, RESIDUE[-1])
    for coefficient in RESIDUE[-2::-1]:
        q = q * square + coefficient
    smooth = whole + rest * square * q
    return f32((scaling * (smooth - offset)).astype(jnp.bfloat16))


def code_kernel(where_ref, head_ref, rest_ref, *refs, strip, first):
    slots, tile, width = rest_ref.shape
    slots += 1
    own_refs, mate_refs = refs[:slots], refs[slots : 2 * slots]
    own_off, mate_off, out_ref, own_wide, mate_wide = refs[2 * slots :]
    per = width // BLOCK
    blocks = own_off.shape[1]
    lane_block = lax.broadcasted_iota(jnp.int32, (blocks, width), 1) // BLOCK
    block = lax.broadcasted_iota(jnp.int32, (blocks, width), 0)
    for s in range(slots):
        pick = (block == lane_block + (first + s * per)).astype(jnp.bfloat16)
        own_wide[s] = jnp.dot(own_off[...], pick, preferred_element_type=jnp.float32)
        mate_wide[s] = jnp.dot(mate_off[...], pick, preferred_element_type=jnp.float32)

    def step(i, carry):
        rows = pl.ds(pl.multiple_of(i * strip, strip), strip)
        for s in range(slots):
            for b in range(per):
                lanes = slice(b * BLOCK, (b + 1) * BLOCK)
                anchor = f32(rest_ref[s - 1, rows, lanes] if s else head_ref[rows, lanes])
                total = coded_strip(anchor, own_refs[s][rows, lanes], own_wide[s, rows, lanes])
                total += coded_strip(anchor, mate_refs[s][rows, lanes], mate_wide[s, rows, lanes])
                out_ref[s, rows, lanes] = total.astype(out_ref.dtype)
        return carry

    lax.fori_loop(0, tile // strip, step, 0)


def code(where, head, rest, weights, mate, own_off, mate_off, group, row):
    slots, rows, width = rest.shape
    slots += 1
    half = weights.shape[0] // 2
    tile = math.gcd(rows, row, TILE)
    strip = math.gcd(tile, STRIP)
    blocks = own_off.shape[1]
    row_of = lambda i, w: w[0] * (half // tile) + row // tile + i
    column = lambda s: 1 + group * slots + s
    in_specs = [
        pl.BlockSpec((tile, width), lambda i, w: (row // tile + i, 0)),
        pl.BlockSpec((slots - 1, tile, width), lambda i, w: (0, i, 0)),
    ]
    in_specs += [pl.BlockSpec((tile, width), lambda i, w, s=s: (row_of(i, w), w[column(s)])) for s in range(slots)]
    in_specs += [pl.BlockSpec((tile, width), lambda i, w, s=s: (i, w[column(s)])) for s in range(slots)]
    in_specs += [
        pl.BlockSpec((tile, blocks), lambda i, w: (row_of(i, w), 0)),
        pl.BlockSpec((tile, blocks), lambda i, w: (row // tile + i, 0)),
    ]
    return pl.pallas_call(
        functools.partial(code_kernel, strip=strip, first=group * slots * (width // BLOCK)),
        out_shape=jax.ShapeDtypeStruct((slots, rows, width), jnp.bfloat16),
        grid_spec=pltpu.PrefetchScalarGridSpec(
            num_scalar_prefetch=1,
            grid=(rows // tile,),
            in_specs=in_specs,
            out_specs=pl.BlockSpec((slots, tile, width), lambda i, w: (0, i, 0)),
            scratch_shapes=[pltpu.VMEM((slots, tile, width), jnp.float32)] * 2,
        ),
        name="code_pair",
        compiler_params=pltpu.CompilerParams(dimension_semantics=("arbitrary",)),
        cost_estimate=pl.CostEstimate(
            flops=80 * slots * rows * width, transcendentals=0, bytes_accessed=8 * slots * rows * width
        ),
    )(where, head, rest, *([weights] * slots), *([mate] * slots), own_off, mate_off)


def merge_kernel(where_ref, *refs, groups):
    fresh, weights_ref, out_ref = refs[:groups], refs[groups], refs[-1]
    slots, _, width = fresh[0].shape
    for g in range(groups):
        for s in range(slots):
            lanes = pl.ds(pl.multiple_of(where_ref[1 + g * slots + s] * width, width), width)
            both = f32(weights_ref[:, lanes]) * mix_share + f32(fresh[g][s]) * (1.0 - mix_share)
            out_ref[:, lanes] = both.astype(out_ref.dtype)


def merge(where, fresh, weights, row, mine, so_far):
    slots, rows, width = fresh[0].shape
    half = weights.shape[0] // 2
    tile = math.gcd(rows, row, MERGE_TILE)

    def place(i, w):
        return ((w[0] if mine else 1 - w[0]) * (half // tile) + row // tile + i, 0)

    full = pl.BlockSpec((tile, weights.shape[1]), place)
    operands = [where, *fresh, weights]
    in_specs = [pl.BlockSpec((slots, tile, width), lambda i, w: (0, i, 0))] * len(fresh) + [full]
    aliases = {}
    if so_far is not None:
        aliases = {len(operands): 0}
        operands.append(so_far)
        in_specs.append(pl.BlockSpec(memory_space=pl.ANY))
    return pl.pallas_call(
        functools.partial(merge_kernel, groups=len(fresh)),
        out_shape=jax.ShapeDtypeStruct(weights.shape, jnp.bfloat16),
        grid_spec=pltpu.PrefetchScalarGridSpec(
            num_scalar_prefetch=1, grid=(rows // tile,), in_specs=in_specs, out_specs=full
        ),
        input_output_aliases=aliases,
        name="merge_rows",
        compiler_params=pltpu.CompilerParams(dimension_semantics=("arbitrary",)),
        cost_estimate=pl.CostEstimate(
            flops=4 * rows * weights.shape[1], transcendentals=0, bytes_accessed=6 * rows * weights.shape[1]
        ),
    )(*operands)


class Line:
    def __init__(self, total, length, stride):
        self.length = length
        self.stride = stride
        self.position = (lax.axis_index("rep") // stride) % length
        self.total = total

    def send(self, array, by):
        def target(i):
            n = (i // self.stride) % self.length
            return i + ((n + by) % self.length - n) * self.stride

        return lax.ppermute(array, "rep", [(i, target(i)) for i in range(self.total)])

    def gather(self, array):
        return [array] + [self.send(array, -d) for d in range(1, self.length)]

    def reduce(self, slots):
        arrived = [self.send(slots[d], d) for d in range(1, self.length)]
        return sum((f32(a) for a in arrived), f32(slots[0]))


def project(hidden, weights):
    share = lax.axis_size("fsdp")
    place = lax.axis_index("fsdp")
    depth = weights.shape[0]
    tokens = hidden.shape[0]

    def columns(at):
        return lax.dynamic_slice(hidden, (0, at % share * depth), (tokens, depth))

    def shifted(array, by):
        return lax.ppermute(array, "fsdp", [(i, (i + by) % share) for i in range(share)])

    gathered = [columns(place)] + [shifted(columns(place + s), s) for s in range(1, share)]
    partial = jnp.dot(jnp.concatenate(gathered), weights, preferred_element_type=jnp.float32)
    parts = [partial[:tokens]] + [shifted(partial[s * tokens : (s + 1) * tokens], -s) for s in range(1, share)]
    return sum(parts[1:], parts[0]).astype(jnp.bfloat16)


def shards(hidden, local_weight, master, momentum, dither):
    weights = local_weight[0]
    rows, columns = weights.shape
    replicas = lax.axis_size("rep")
    chips = replicas // 2
    x_length = 2 ** int(math.log2(chips) / 2)
    z_length = chips // x_length
    core = lax.axis_index("rep") % 2
    x_line = Line(replicas, x_length, 2)
    z_line = Line(replicas, z_length, 2 * x_length)
    half = rows // 2
    width = columns // chips
    mine, theirs = core * half, (1 - core) * half

    def swap(array):
        return lax.ppermute(array, "rep", [(i, i ^ 1) for i in range(replicas)])

    def halves(array, start, count=half):
        return lax.dynamic_slice(array, (start, 0), (count, array.shape[1]))

    def beside(own, other):
        return jnp.where(core == 0, jnp.concatenate([own, other], 1), jnp.concatenate([other, own], 1))

    edges = [half * sum(SHARES[:i]) // sum(SHARES) for i in range(CHUNKS + 1)]
    parts = [slice(a, b) for a, b in zip(edges, edges[1:])]

    rounded = [halves(master, start).astype(jnp.bfloat16) for start in (mine, theirs)]
    anchor = beside(rounded[0], swap(rounded[1]))

    heads = x_line.gather(anchor)
    rests = []
    for part in parts:
        pieces = z_line.gather(anchor[part])
        rests.append(x_line.gather(jnp.stack(pieces[1:])))

    d = jnp.arange(z_length, dtype=jnp.int32)[None, :]
    e = jnp.arange(x_length, dtype=jnp.int32)[:, None]
    places = (((z_line.position + d) % z_length) * x_length + (x_line.position + e) % x_length).reshape(-1)
    where = jnp.concatenate([core[None].astype(jnp.int32), places])

    offset = (f32(dither[0]) + 0.5) / 16.0 - 0.5
    block_places = (places[:, None] * (width // BLOCK) + jnp.arange(width // BLOCK)[None, :]).reshape(-1)
    pick = jnp.arange(offset.shape[1])[:, None] == block_places[None, :]
    offset = jnp.dot(offset.astype(jnp.bfloat16), pick.astype(jnp.bfloat16), preferred_element_type=jnp.float32)
    offset = offset.astype(jnp.bfloat16)
    mate_offset = swap(halves(offset, theirs))
    mates = [swap(halves(weights, theirs + part.start, part.stop - part.start)) for part in parts]
    pair_master = beside(halves(master, mine), swap(halves(master, theirs)))
    pair_momentum = beside(halves(momentum, mine), swap(halves(momentum, theirs)))
    key_values = project(hidden, weights)

    masters, momenta, fresh, swapped = [], [], [], []
    for i, part in enumerate(parts):
        sums = [None] * x_length
        for g in reversed(range(x_length)):
            sums[g] = code(where, heads[g], rests[i][g], weights, mates[i], offset, mate_offset, g, part.start)
        arrived = [x_line.send(sums[e], e) for e in range(1, x_length)]
        summed = [
            sum((f32(a[k]) for a in arrived), f32(sums[0][k])).astype(jnp.bfloat16) for k in range(z_length)
        ]
        total = z_line.reduce(summed)
        old_master, old_momentum, *_ = lax.optimization_barrier((pair_master[part], pair_momentum[part], *masters[-1:]))
        averaged = total / replicas
        new_momentum = momentum_keep * old_momentum + averaged
        new_master = old_master - outer_rate * (averaged + momentum_keep * new_momentum)
        masters.append(new_master)
        momenta.append(new_momentum)
        pieces = z_line.gather(new_master.astype(jnp.bfloat16))
        fresh.append(x_line.gather(jnp.stack(pieces)))
        swapped.append([None] * x_length)
        for g, group in enumerate(fresh[-1]):
            swapped[-1][g] = swap(group)

    def home(pieces):
        pair = jnp.concatenate(pieces)
        own = pair.shape[1] // 2
        left, right = pair[:, :own], pair[:, own:]
        keep, give = jnp.where(core == 0, left, right), jnp.where(core == 0, right, left)
        got = swap(give)
        return jnp.where(core == 0, jnp.concatenate([keep, got]), jnp.concatenate([got, keep]))

    final_master, final_momentum = home(masters), home(momenta)
    new_local = None
    for i, part in enumerate(parts):
        new_local = merge(where, fresh[i], weights, part.start, True, new_local)
        new_local = merge(where, swapped[i], weights, part.start, False, new_local)
    return (key_values, final_master, final_momentum, new_local[None])


def solution(mesh):
    return jax.shard_map(
        shards,
        mesh=mesh,
        in_specs=(
            P(("rep", "fsdp"), None),
            P("rep", "fsdp", None),
            P("fsdp", "rep"),
            P("fsdp", "rep"),
            P("rep", "fsdp", None),
        ),
        out_specs=(
            P(("rep", "fsdp"), None),
            P("fsdp", "rep"),
            P("fsdp", "rep"),
            P("rep", "fsdp", None),
        ),
        check_vma=False,
    )
```

```python
import functools
import math

import jax
import jax.numpy as jnp
from jax import lax
from jax.experimental import pallas as pl
from jax.experimental.pallas import tpu as pltpu
from jax.sharding import PartitionSpec as P

BLOCK = 128
momentum_keep = 0.9
outer_rate = 0.7
mix_share = 0.5

RESIDUE = (6.579735248418329, -12.987673932477895, 12.201508758913876, -6.6188575657590425, 2.0504529183602735)

SHARES = (1, 1, 1, 1)
CHUNKS = len(SHARES)
TILE = 256
STRIP = 32
MERGE_TILE = 256


def f32(array):
    return array.astype(jnp.float32)


def coded_strip(anchor, weights, offset):
    delta = anchor - f32(weights)
    scaling = (jnp.max(jnp.abs(delta), axis=1, keepdims=True) + 1e-06) * (1.0 / 7.0)
    levels = jnp.clip(delta * (1.0 / scaling) + offset, -8.0, 7.0)
    whole = jnp.round(levels)
    rest = levels - whole
    square = rest * rest
    q = jnp.full_like(square, RESIDUE[-1])
    for coefficient in RESIDUE[-2::-1]:
        q = q * square + coefficient
    smooth = whole + rest * square * q
    return f32((scaling * (smooth - offset)).astype(jnp.bfloat16))


def code_kernel(where_ref, head_ref, rest_ref, *refs, strip, first):
    slots, tile, width = rest_ref.shape
    slots += 1
    own_refs, mate_refs = refs[:slots], refs[slots : 2 * slots]
    own_off, mate_off, out_ref, own_wide, mate_wide = refs[2 * slots :]
    per = width // BLOCK
    blocks = own_off.shape[1]
    lane_block = lax.broadcasted_iota(jnp.int32, (blocks, width), 1) // BLOCK
    block = lax.broadcasted_iota(jnp.int32, (blocks, width), 0)
    for s in range(slots):
        pick = (block == lane_block + (first + s * per)).astype(jnp.bfloat16)
        own_wide[s] = jnp.dot(own_off[...], pick, preferred_element_type=jnp.float32)
        mate_wide[s] = jnp.dot(mate_off[...], pick, preferred_element_type=jnp.float32)

    def step(i, carry):
        rows = pl.ds(pl.multiple_of(i * strip, strip), strip)
        for s in range(slots):
            for b in range(per):
                lanes = slice(b * BLOCK, (b + 1) * BLOCK)
                anchor = f32(rest_ref[s - 1, rows, lanes] if s else head_ref[rows, lanes])
                total = coded_strip(anchor, own_refs[s][rows, lanes], own_wide[s, rows, lanes])
                total += coded_strip(anchor, mate_refs[s][rows, lanes], mate_wide[s, rows, lanes])
                out_ref[s, rows, lanes] = total.astype(out_ref.dtype)
        return carry

    lax.fori_loop(0, tile // strip, step, 0)


def code(where, head, rest, weights, mate, own_off, mate_off, group, row):
    slots, rows, width = rest.shape
    slots += 1
    half = weights.shape[0] // 2
    tile = math.gcd(rows, row, TILE)
    strip = math.gcd(tile, STRIP)
    blocks = own_off.shape[1]
    row_of = lambda i, w: w[0] * (half // tile) + row // tile + i
    column = lambda s: 1 + group * slots + s
    in_specs = [
        pl.BlockSpec((tile, width), lambda i, w: (row // tile + i, 0)),
        pl.BlockSpec((slots - 1, tile, width), lambda i, w: (0, i, 0)),
    ]
    in_specs += [pl.BlockSpec((tile, width), lambda i, w, s=s: (row_of(i, w), w[column(s)])) for s in range(slots)]
    in_specs += [pl.BlockSpec((tile, width), lambda i, w, s=s: (i, w[column(s)])) for s in range(slots)]
    in_specs += [
        pl.BlockSpec((tile, blocks), lambda i, w: (row_of(i, w), 0)),
        pl.BlockSpec((tile, blocks), lambda i, w: (row // tile + i, 0)),
    ]
    return pl.pallas_call(
        functools.partial(code_kernel, strip=strip, first=group * slots * (width // BLOCK)),
        out_shape=jax.ShapeDtypeStruct((slots, rows, width), jnp.bfloat16),
        grid_spec=pltpu.PrefetchScalarGridSpec(
            num_scalar_prefetch=1,
            grid=(rows // tile,),
            in_specs=in_specs,
            out_specs=pl.BlockSpec((slots, tile, width), lambda i, w: (0, i, 0)),
            scratch_shapes=[pltpu.VMEM((slots, tile, width), jnp.float32)] * 2,
        ),
        name="code_pair",
        compiler_params=pltpu.CompilerParams(dimension_semantics=("arbitrary",)),
        cost_estimate=pl.CostEstimate(
            flops=80 * slots * rows * width, transcendentals=0, bytes_accessed=8 * slots * rows * width
        ),
    )(where, head, rest, *([weights] * slots), *([mate] * slots), own_off, mate_off)


def merge_kernel(where_ref, *refs, groups):
    fresh, weights_ref, out_ref = refs[:groups], refs[groups], refs[-1]
    at = 1
    for group in fresh:
        slots, _, width = group.shape
        for s in range(slots):
            lanes = pl.ds(pl.multiple_of(where_ref[at] * width, width), width)
            both = f32(weights_ref[:, lanes]) * mix_share + f32(group[s]) * (1.0 - mix_share)
            out_ref[:, lanes] = both.astype(out_ref.dtype)
            at += 1


def merge(where, fresh, weights, row, mine, so_far):
    _, rows, width = fresh[0].shape
    half = weights.shape[0] // 2
    tile = math.gcd(rows, row, MERGE_TILE)

    def place(i, w):
        return ((w[0] if mine else 1 - w[0]) * (half // tile) + row // tile + i, 0)

    full = pl.BlockSpec((tile, weights.shape[1]), place)
    operands = [where, *fresh, weights]
    in_specs = [pl.BlockSpec((group.shape[0], tile, width), lambda i, w: (0, i, 0)) for group in fresh] + [full]
    aliases = {}
    if so_far is not None:
        aliases = {len(operands): 0}
        operands.append(so_far)
        in_specs.append(pl.BlockSpec(memory_space=pl.ANY))
    return pl.pallas_call(
        functools.partial(merge_kernel, groups=len(fresh)),
        out_shape=jax.ShapeDtypeStruct(weights.shape, jnp.bfloat16),
        grid_spec=pltpu.PrefetchScalarGridSpec(
            num_scalar_prefetch=1, grid=(rows // tile,), in_specs=in_specs, out_specs=full
        ),
        input_output_aliases=aliases,
        name="merge_rows",
        compiler_params=pltpu.CompilerParams(dimension_semantics=("arbitrary",)),
        cost_estimate=pl.CostEstimate(
            flops=4 * rows * weights.shape[1], transcendentals=0, bytes_accessed=6 * rows * weights.shape[1]
        ),
    )(*operands)


class Line:
    def __init__(self, total, length, stride):
        self.length = length
        self.stride = stride
        self.position = (lax.axis_index("rep") // stride) % length
        self.total = total

    def send(self, array, by):
        def target(i):
            n = (i // self.stride) % self.length
            return i + ((n + by) % self.length - n) * self.stride

        return lax.ppermute(array, "rep", [(i, target(i)) for i in range(self.total)])

    def gather(self, array):
        return [array] + [self.send(array, -d) for d in range(1, self.length)]

    def reduce(self, slots):
        arrived = [self.send(slots[d], d) for d in range(1, self.length)]
        return sum((f32(a) for a in arrived), f32(slots[0]))


def project(hidden, weights):
    share = lax.axis_size("fsdp")
    place = lax.axis_index("fsdp")
    depth = weights.shape[0]
    tokens = hidden.shape[0]

    def columns(at):
        return lax.dynamic_slice(hidden, (0, at % share * depth), (tokens, depth))

    def shifted(array, by):
        return lax.ppermute(array, "fsdp", [(i, (i + by) % share) for i in range(share)])

    gathered = [columns(place)] + [shifted(columns(place + s), s) for s in range(1, share)]
    partial = jnp.dot(jnp.concatenate(gathered), weights, preferred_element_type=jnp.float32)
    parts = [partial[:tokens]] + [shifted(partial[s * tokens : (s + 1) * tokens], -s) for s in range(1, share)]
    return sum(parts[1:], parts[0]).astype(jnp.bfloat16)


def shards(hidden, local_weight, master, momentum, dither):
    weights = local_weight[0]
    rows, columns = weights.shape
    replicas = lax.axis_size("rep")
    chips = replicas // 2
    x_length = 2 ** int(math.log2(chips) / 2)
    z_length = chips // x_length
    core = lax.axis_index("rep") % 2
    x_line = Line(replicas, x_length, 2)
    z_line = Line(replicas, z_length, 2 * x_length)
    half = rows // 2
    width = columns // chips
    mine, theirs = core * half, (1 - core) * half

    def swap(array):
        return lax.ppermute(array, "rep", [(i, i ^ 1) for i in range(replicas)])

    def halves(array, start, count=half):
        return lax.dynamic_slice(array, (start, 0), (count, array.shape[1]))

    def beside(own, other):
        return jnp.where(core == 0, jnp.concatenate([own, other], 1), jnp.concatenate([other, own], 1))

    edges = [half * sum(SHARES[:i]) // sum(SHARES) for i in range(CHUNKS + 1)]
    parts = [slice(a, b) for a, b in zip(edges, edges[1:])]

    rounded = [halves(master, start).astype(jnp.bfloat16) for start in (mine, theirs)]
    other = swap(rounded[1])
    anchor = beside(rounded[0], other)

    heads = x_line.gather(anchor)
    rests = []
    for part in parts:
        pieces = z_line.gather(beside(rounded[0][part], other[part]))
        rests.append(x_line.gather(jnp.stack(pieces[1:])))

    d = jnp.arange(z_length, dtype=jnp.int32)[None, :]
    e = jnp.arange(x_length, dtype=jnp.int32)[:, None]
    places = (((z_line.position + d) % z_length) * x_length + (x_line.position + e) % x_length).reshape(-1)
    where = jnp.concatenate([core[None].astype(jnp.int32), places])

    offset = (f32(dither[0]) + 0.5) / 16.0 - 0.5
    block_places = (places[:, None] * (width // BLOCK) + jnp.arange(width // BLOCK)[None, :]).reshape(-1)
    pick = jnp.arange(offset.shape[1])[:, None] == block_places[None, :]
    offset = jnp.dot(offset.astype(jnp.bfloat16), pick.astype(jnp.bfloat16), preferred_element_type=jnp.float32)
    offset = offset.astype(jnp.bfloat16)
    mate_offset = swap(halves(offset, theirs))
    mates = [swap(halves(weights, theirs + part.start, part.stop - part.start)) for part in parts]
    master, momentum, _ = lax.optimization_barrier((master, momentum, rests[0][0]))
    pair_master = beside(halves(master, mine), swap(halves(master, theirs)))
    pair_momentum = beside(halves(momentum, mine), swap(halves(momentum, theirs)))
    key_values = project(hidden, weights)

    masters, momenta, fresh, swapped = [], [], [], []
    for i, part in enumerate(parts):
        sums = [None] * x_length
        for g in reversed(range(x_length)):
            sums[g] = code(where, heads[g], rests[i][g], weights, mates[i], offset, mate_offset, g, part.start)
        arrived = [x_line.send(sums[e], e) for e in range(1, x_length)]
        summed = [
            sum((f32(a[k]) for a in arrived), f32(sums[0][k])).astype(jnp.bfloat16) for k in range(z_length)
        ]
        total = z_line.reduce(summed)
        old_master, old_momentum, *_ = lax.optimization_barrier((pair_master[part], pair_momentum[part], *masters[-1:]))
        averaged = total / replicas
        new_momentum = momentum_keep * old_momentum + averaged
        new_master = old_master - outer_rate * (averaged + momentum_keep * new_momentum)
        masters.append(new_master)
        momenta.append(new_momentum)
        pieces = z_line.gather(new_master.astype(jnp.bfloat16))
        ends = [[] for _ in range(x_length)]
        if i == CHUNKS - 1:
            for g, end in enumerate(x_line.gather(pieces[0][None])):
                ends[g].append(end)
        for g, end in enumerate(x_line.gather(jnp.stack(pieces[len(ends[0]) :]))):
            ends[g].append(end)
        swapped.append([])
        for group in ends:
            for end in group:
                swapped[-1].append(swap(end))
        fresh.append([end for group in ends for end in group])

    def home(pieces):
        pair = jnp.concatenate(pieces)
        own = pair.shape[1] // 2
        left, right = pair[:, :own], pair[:, own:]
        keep, give = jnp.where(core == 0, left, right), jnp.where(core == 0, right, left)
        got = swap(give)
        return jnp.where(core == 0, jnp.concatenate([keep, got]), jnp.concatenate([got, keep]))

    final_master, final_momentum = home(masters), home(momenta)
    new_local = None
    for i, part in enumerate(parts):
        new_local = merge(where, fresh[i], weights, part.start, True, new_local)
        new_local = merge(where, swapped[i], weights, part.start, False, new_local)
    return (key_values, final_master, final_momentum, new_local[None])


def solution(mesh):
    return jax.shard_map(
        shards,
        mesh=mesh,
        in_specs=(
            P(("rep", "fsdp"), None),
            P("rep", "fsdp", None),
            P("fsdp", "rep"),
            P("fsdp", "rep"),
            P("rep", "fsdp", None),
        ),
        out_specs=(
            P(("rep", "fsdp"), None),
            P("fsdp", "rep"),
            P("fsdp", "rep"),
            P("rep", "fsdp", None),
        ),
        check_vma=False,
    )
```
